32 devices in a mesh: dec: 2 (over x), ada: 16 (over z, y, core).
Axes of the slice: x: 2, y: 2, z: 4, core: 2. Of those that a mesh axis runs over, the one named last changes fastest.
Arguments:
- inputs: bfloat16 [4, 64, 8192], P(None, ('dec', 'ada')), may hold values from -6 to 6
- query_weight: bfloat16 [8192, 8192], P(None, 'ada'), may hold values from -0.0625 to 0.0625
- adapter_down: bfloat16 [32, 8192, 64], P(('dec', 'ada')), may hold values from -0.0625 to 0.0625
- adapter_up: bfloat16 [32, 64, 8192], P(('dec', 'ada')), may hold values from -0.75 to 0.75
- adapter_ids: int32 [64, 1], P(('dec', 'ada')), may hold values from 0 to 15; in each aligned block of 32 rows (0 to 31, 32 to 63, ...) at most 4 rows name the same one
- new_cache: bfloat16 [4, 64, 2, 1024], P(None, ('dec', 'ada')), may hold values from -9 to 9
- cache_pool: bfloat16 [256, 2, 16, 1024], P(('dec', 'ada')), may hold values from -400 to 400
- page_table: int32 [64, 4], P(('dec', 'ada')), may hold values from 0 to 15, as said below
- lengths: int32 [64], P(('dec', 'ada')), may hold values from 1 to 64, as said below
Outputs:
- attended: bfloat16 [4, 64, 8192], P(None, ('dec', 'ada'))
The draws below stay inside these ranges and needn't reach their ends.
Inputs may be any that keep to these rules, and one draw needn't show every extreme that they name: `adapter_ids`: in each aligned block of 32 rows (one decode group) no id is named by more than 4 rows, a bound that some block reaches. `page_table`: entries j >= ceil(lengths[r] / 16) are unused. Among rows with the same (r % 32) // 2, the live entries are all different. `lengths`: among rows with the same (r % 32) // 2, one reaches 64.
All inputs are finite; a program needn't handle non-finite values.
Results may differ from the reference program's by a relative error of at most 0.007.
The reference program's roundings to bfloat16 on the way count: a program that leaves them out, or rounds other values in their place, can miss the bound.
Values may be sent and summed in bfloat16 or wider, within the bound.
A program may use at most 64 MiB of HBM per device.

```python
import math
from functools import reduce
import jax
import jax.numpy as jnp
import numpy as np
from jax import lax

D = 8192
HEADS = 64
KVH = 8
HD = 128
RANK = 64
STEPS = 4
PAGE = 16
MAXP = 4
ROW_DEV = 2
CAP = 4
ROWS = 64
GROUP_ROWS = 32
GROUP_ADP = 16
ADAPTERS = 32
POOL_DEV = 8
POOL_GROUP = 128
POOLS = 256
N_DEC = 2
N_ADA = 16


def page_layout(key):
    column_rows = N_DEC * ROW_DEV
    total = N_DEC * POOL_DEV
    key_count, key_forced, key_extra, key_order = jax.random.split(jax.random.fold_in(key, 7), 4)
    counts = jax.random.randint(key_count, (N_ADA, column_rows), 1, MAXP + 1)
    forced = jax.random.randint(key_forced, (N_ADA, 1), 0, column_rows)
    position = jnp.arange(column_rows)[None, :]
    counts = jnp.where(position == forced, MAXP, counts)
    extra = jax.random.randint(key_extra, (N_ADA, column_rows), 0, PAGE)
    lengths = jnp.where(position == forced, MAXP * PAGE, (counts - 1) * PAGE + 1 + extra)
    orders = jax.vmap(lambda subkey: jax.random.permutation(subkey, total))(jax.random.split(key_order, N_ADA))
    starts = jnp.cumsum(counts, axis=1) - counts
    index = (starts[:, :, None] + jnp.arange(MAXP)[None, None, :]) % total
    table = jax.vmap(lambda order, where: order[where])(orders, index)
    table = jnp.transpose(table.reshape(N_ADA, N_DEC, ROW_DEV, MAXP), (1, 0, 2, 3)).reshape(ROWS, MAXP)
    lengths = jnp.transpose(lengths.reshape(N_ADA, N_DEC, ROW_DEV), (1, 0, 2)).reshape(ROWS)
    return (table.astype(jnp.int32), lengths.astype(jnp.int32))


def draw_page_table(key, part):
    return page_layout(key)[0]


def draw_lengths(key, part):
    return page_layout(key)[1]


def draw_cache_pool(key, part):
    width = KVH * HD
    key_keys, key_flag, key_scale, key_vals = jax.random.split(jax.random.fold_in(key, 11), 4)
    halves = jnp.clip(jax.random.normal(key_keys, (POOLS, 1, PAGE // 2, 1, width), jnp.float32), -6.0, 6.0)
    scale = jnp.exp(jax.random.uniform(key_scale, (POOLS, 1, 1, width), jnp.float32, -1.4, 1.4))
    other = jnp.clip(jax.random.normal(key_flag, (POOLS, 1, PAGE // 2, 1, width), jnp.float32), -6.0, 6.0)
    keys = jnp.concatenate([halves, other], axis=3).reshape(POOLS, 1, PAGE, width) * scale
    values = jnp.clip(jax.random.normal(key_vals, (POOLS, 1, PAGE, width), jnp.float32), -6.0, 6.0)
    return jnp.concatenate([keys, values], axis=1).astype(jnp.bfloat16)


def block_levels(own_key, dims, shards, low, high):
    level, own = 1.0, jax.random.fold_in(own_key, 6)
    for axis_at, blocks in shards:
        draws = jnp.exp(jax.random.uniform(jax.random.fold_in(own, axis_at), (blocks,), jnp.float32, low / len(shards), high / len(shards)))
        level = level * jnp.repeat(draws, dims[axis_at] // blocks).reshape([-1 if axis == axis_at else 1 for axis in range(len(dims))])
    return level


def shared_out(rng, own, number, rows, number_of, top, bound, skew):
    order = jax.random.permutation(rng, number_of)
    packed, common = portions_of(number_of, rows * top, bound, skew, True), portions_of(number_of, rows * top, bound, skew, False)
    places = jnp.arange(number_of)

    def named(tallies, turn):
        used = int((tallies > 0).sum())
        fixed = max(1, used // 4)
        moved = fixed + (places - fixed + turn * (used - fixed)) % max(1, number_of - fixed)
        return jnp.zeros((number_of,), jnp.int32).at[order[jnp.where(places < fixed, places, moved)]].set(jnp.asarray(tallies, jnp.int32))

    tallies = jnp.where(number % 4 == 0, named(packed, number // 4), named(common, number - number // 4 - 1))
    mixed = jax.random.permutation(jax.random.fold_in(own, 3), number_of)
    giver, sink = mixed[0:number_of // 2 * 2:2], mixed[1:number_of // 2 * 2:2]
    margin = jnp.minimum(tallies[giver] - 1, bound - tallies[sink]) // 2
    margin = jnp.where((giver == order[0]) | (sink == order[0]) | (tallies[sink] == 0), 0, jnp.maximum(margin, 0))
    moved = jax.random.randint(jax.random.fold_in(own, 4), (number_of // 2,), 0, 1 << 20) % (margin + 1)
    tallies = tallies.at[giver].add(-moved).at[sink].add(moved)
    labels = jnp.searchsorted(jnp.cumsum(tallies), jnp.arange(rows * top), side="right").astype(jnp.int32)
    listing = labels.reshape(top, rows).T
    listing = listing[jax.random.permutation(jax.random.fold_in(own, 1), rows)]
    turn = jax.random.randint(jax.random.fold_in(own, 2), (rows, 1), 0, top)
    return jnp.take_along_axis(listing, (jnp.arange(top)[None, :] + turn) % top, axis=1)


def portions_of(number_of, total, bound, lean, full):
    weights = [(1 << 20) // math.isqrt(grade ** lean) + 1 for grade in range(1, number_of + 1)]
    largest = bound if full else min(bound, max(-(-total // number_of), total * weights[0] // sum(weights)))
    least = 1 if total - largest >= number_of - 1 else 0
    holding, rest = [largest] + [least] * (number_of - 1), total - largest - least * (number_of - 1)
    while rest > 0:
        free = [i for i in range(1, number_of) if holding[i] < largest] or [i for i in range(1, number_of) if holding[i] < bound]
        whole, remaining = sum([weights[i] for i in free]), rest
        for i in free:
            addition = min(bound - holding[i], max(1, remaining * weights[i] // whole), rest)
            holding[i] = holding[i] + addition
            rest = rest - addition
    return np.array(holding)


def gaussian(key, shape, spread, limit, pieces=(), kind=jnp.bfloat16):
    drawn = jax.random.normal(key, shape, jnp.float32) * spread
    if len(pieces) > 0:
        drawn = block_levels(key, shape, pieces, -0.22, 0.18) * drawn
    return jnp.clip(drawn, min=-limit, max=limit).astype(kind)


def setup_inputs(seed: int = 0) -> dict:
    arg_keys = jax.random.split(jax.random.key(seed), 10)
    inputs = gaussian(arg_keys[0], (STEPS, ROWS, D), 1.0, 6.0, ((1, 32),))
    query_weight = gaussian(arg_keys[1], (D, D), D ** -0.5, 0.0625, ((1, 16),))
    adapter_down = gaussian(arg_keys[2], (ADAPTERS, D, RANK), D ** -0.5, 0.0625, ((0, 32),))
    adapter_up = gaussian(arg_keys[3], (ADAPTERS, RANK, D), RANK ** -0.5, 0.75, ((0, 32),))
    adapter_ids_keys = jax.random.split(jax.random.fold_in(arg_keys[4], 1), ROWS // GROUP_ROWS)
    adapter_ids_turns = jax.random.permutation(jax.random.fold_in(arg_keys[4], 3), ROWS // GROUP_ROWS)
    adapter_ids = jax.vmap(lambda own, number: shared_out(jax.random.fold_in(arg_keys[4], 2), own, number, GROUP_ROWS, GROUP_ADP, 1, CAP, 1))(adapter_ids_keys, adapter_ids_turns).reshape((ROWS, 1))
    new_cache = gaussian(arg_keys[5], (STEPS, ROWS, 2, KVH * HD), 1.5, 9.0, ((1, 32),))
    cache_pool = draw_cache_pool(jax.random.fold_in(arg_keys[9], 71), 0)
    page_table = draw_page_table(jax.random.fold_in(arg_keys[9], 71), 0)
    lengths = draw_lengths(jax.random.fold_in(arg_keys[9], 71), 0)
    return {"inputs": inputs, "query_weight": query_weight, "adapter_down": adapter_down, "adapter_up": adapter_up, "adapter_ids": adapter_ids, "new_cache": new_cache, "cache_pool": cache_pool, "page_table": page_table, "lengths": lengths}


NEGATIVE = -1e+30
HIGH = lax.Precision.HIGHEST

def cache_part(query, keys, values, live):
    scale = 1.0 / math.sqrt(query.shape[-1])
    scores = jnp.einsum('trkgd,rpkd->trkgp', query.astype(jnp.float32), keys.astype(jnp.float32), precision=HIGH) * scale
    mask = live[None, :, None, None, :]
    scores = jnp.where(mask, scores, NEGATIVE)
    top = lax.optimization_barrier(jnp.max(scores, axis=-1))
    weights = jnp.where(mask, jnp.exp(scores - top[..., None]), 0.0)
    numerator = jnp.einsum('trkgp,rpkd->trkgd', weights, values.astype(jnp.float32), precision=HIGH)
    return (numerator, top, lax.optimization_barrier(jnp.sum(weights, axis=-1)))

def fresh_part(query, new_entries):
    steps, rows, kv_heads, group, head_dim = query.shape
    scale = 1.0 / math.sqrt(head_dim)
    keys = new_entries[:, :, 0].reshape(new_entries.shape[0], rows, kv_heads, head_dim)
    values = new_entries[:, :, 1].reshape(new_entries.shape[0], rows, kv_heads, head_dim)
    scores = jnp.einsum('trkgd,urkd->trkgu', query.astype(jnp.float32), keys.astype(jnp.float32), precision=HIGH) * scale
    allowed = (jnp.arange(new_entries.shape[0])[None, :] <= jnp.arange(steps)[:, None])[:, None, None, None, :]
    scores = jnp.where(allowed, scores, NEGATIVE)
    top = lax.optimization_barrier(jnp.max(scores, axis=-1))
    weights = jnp.where(allowed, jnp.exp(scores - top[..., None]), 0.0)
    numerator = jnp.einsum('trkgu,urkd->trkgd', weights, values.astype(jnp.float32), precision=HIGH)
    return (numerator, top, lax.optimization_barrier(jnp.sum(weights, axis=-1)))

def finish(parts):
    top = reduce(jnp.maximum, [part[1] for part in parts])
    numerator = sum((part[0] * jnp.exp(part[1] - top)[..., None] for part in parts))
    total = sum((part[2] * jnp.exp(part[1] - top) for part in parts))
    return (numerator / total[..., None]).astype(jnp.bfloat16)

def reference(inputs, query_weight, adapter_down, adapter_up, adapter_ids, new_cache, cache_pool, page_table, lengths):
    base_output = jnp.dot(inputs.reshape(STEPS * ROWS, D), query_weight, preferred_element_type=jnp.float32).reshape(STEPS, ROWS, D)

    def one_block(block):
        first = (block * ROW_DEV).astype(jnp.int32)
        rows = first + jnp.arange(ROW_DEV, dtype=jnp.int32)
        input_block = lax.dynamic_slice_in_dim(inputs, first, ROW_DEV, 1)
        base_block = lax.dynamic_slice_in_dim(base_output, first, ROW_DEV, 1)
        entry = rows // GROUP_ROWS * GROUP_ADP + adapter_ids[rows, 0]
        down = adapter_down[entry]
        upward = adapter_up[entry]
        shrink = jnp.einsum('trd,rdk->trk', input_block.astype(jnp.float32), down.astype(jnp.float32), precision=HIGH).astype(jnp.bfloat16)
        delta = jnp.einsum('trk,rkd->trd', shrink.astype(jnp.float32), upward.astype(jnp.float32), precision=HIGH).astype(jnp.bfloat16)
        query = (base_block + delta.astype(jnp.float32)).astype(jnp.bfloat16)
        query = query.reshape(STEPS, ROW_DEV, KVH, HEADS // KVH, HD)
        table = page_table[rows]
        column = (rows % GROUP_ROWS // ROW_DEV)[:, None]
        slot = table // POOL_DEV * POOL_GROUP + column * POOL_DEV + table % POOL_DEV
        pages = cache_pool[slot]
        keys = pages[:, :, 0].reshape(ROW_DEV, MAXP * PAGE, KVH, HD)
        values = pages[:, :, 1].reshape(ROW_DEV, MAXP * PAGE, KVH, HD)
        live = jnp.arange(MAXP * PAGE, dtype=jnp.int32)[None, :] < lengths[rows][:, None]
        new_block = lax.dynamic_slice_in_dim(new_cache, first, ROW_DEV, 1)
        parts = [cache_part(query, keys, values, live), fresh_part(query, new_block)]
        return finish(parts).reshape(STEPS, ROW_DEV, D)
    outputs = lax.map(one_block, jnp.arange(ROWS // ROW_DEV, dtype=jnp.int32))
    return jnp.transpose(outputs, (1, 0, 2, 3)).reshape(STEPS, ROWS, D)
```

```python
import functools
import math

import jax
import jax.numpy as jnp
from jax import lax
from jax.experimental import pallas as pl
from jax.experimental.pallas import tpu as pltpu
from jax.sharding import PartitionSpec as P

HD = 128
CAP = 4
LANES = 128
CHUNKS = 4
NEGATIVE = -1e30
MESH = pl.DeviceIdType.MESH
F32 = jnp.float32
BF16 = jnp.bfloat16


def nt_dot(a, b):
    return lax.dot_general(a, b, (((1,), (1,)), ((), ())), preferred_element_type=F32)


def iota(shape, axis):
    return lax.broadcasted_iota(jnp.int32, shape, axis)


def kernel(
    n,
    n_dec,
    x_ref,
    w_hbm,
    down_hbm,
    up_hbm,
    ids_ref,
    new_ref,
    pool_hbm,
    table_ref,
    len_ref,
    out_ref,
    *scratch,
):
    gathered = scratch[:CHUNKS]
    (
        w_ref, down_ref, up_ref, pages, base, shrink, d_send, d_recv, q_send, q_recv, keys, values,
        w_sem, down_sem, up_sem, pool_sem, pool_send, pool_recv,
        up_send, low_send, across_send, side_send, g_recv, ds_sem, dr_sem, qs_sem, qr_sem,
    ) = scratch[CHUNKS:]
    ada, dec = lax.axis_index("ada"), lax.axis_index("dec")
    steps, rows, width = x_ref.shape
    part = width // CHUNKS
    block = steps * rows
    total = n * block
    head_cols = w_ref.shape[1]
    slots = steps * CAP
    span = n // 4
    o, m, c = ada // 4, (ada // 2) % 2, ada % 2
    sibling = ada + 1 - 2 * c
    opposite = ada + 2 - 4 * m
    pool_local = pool_hbm.shape[0]

    def w_copy(k):
        where = pl.ds(k * part, part)
        return pltpu.make_async_copy(w_hbm.at[where], w_ref.at[where], w_sem.at[k])

    down_copy = pltpu.make_async_copy(down_hbm, down_ref, down_sem)
    up_copy = pltpu.make_async_copy(up_hbm, up_ref, up_sem)
    own_pages = pages.at[pl.ds(dec * pool_local, pool_local)]
    pool_copy = pltpu.make_async_copy(pool_hbm, own_pages, pool_sem)

    mine = jnp.concatenate([x_ref[t].astype(F32) for t in range(steps)], axis=0).astype(BF16)
    row_of = iota((block, LANES), 0) % rows
    id_block = jnp.zeros((block, LANES), F32)
    for r in range(rows):
        id_block = jnp.where(row_of == r, ids_ref[r].astype(F32), id_block)
    for k in range(CHUNKS):
        gathered[k][ada, :, 0:part] = mine[:, k * part : (k + 1) * part]
    gathered[0][ada, :, part : part + LANES] = id_block.astype(BF16)

    barrier = pltpu.get_barrier_semaphore()
    for d in range(1, n):
        pl.semaphore_signal(
            barrier, inc=1, device_id={"ada": lax.rem(ada + d, n)}, device_id_type=MESH
        )
    for d in range(1, n_dec):
        pl.semaphore_signal(
            barrier, inc=1, device_id={"dec": lax.rem(dec + d, n_dec)}, device_id_type=MESH
        )
    w_copy(0).start()
    down_copy.start()
    for k in range(1, CHUNKS):
        w_copy(k).start()
    up_copy.start()
    pool_copy.start()
    pl.semaphore_wait(barrier, n - 1 + n_dec - 1)

    def relay(k, source, send_sem, peer):
        return pltpu.make_async_remote_copy(
            src_ref=gathered[k].at[source],
            dst_ref=gathered[k].at[source],
            send_sem=send_sem,
            recv_sem=g_recv.at[k, source],
            device_id={"ada": peer},
            device_id_type=MESH,
        )

    def arrived(k, source):
        relay(k, source, side_send.at[k, 0], sibling).wait_recv()

    def upward(k, line):
        return relay(k, line * 4 + m * 2 + c, up_send.at[k, line], ada + 4)

    def downward(k, line):
        return relay(k, line * 4 + m * 2 + c, low_send.at[k, line], ada - 4)

    def across(k, line):
        return relay(k, line * 4 + m * 2 + c, across_send.at[k, line], opposite)

    def sideways(k, line, column):
        return relay(
            k, line * 4 + column * 2 + c, side_send.at[k, line * 2 + column], sibling
        )

    def send_own(k):
        across(k, o).start()

        @pl.when(o < span - 1)
        def _():
            upward(k, o).start()

        @pl.when(o > 0)
        def _():
            downward(k, o).start()

        sideways(k, o, m).start()

    def line_wave(k):
        for distance in range(1, span):
            below, above = o - distance, o + distance

            @pl.when(below >= 0)
            def _():
                arrived(k, below * 4 + m * 2 + c)
                across(k, below).start()

                @pl.when(o < span - 1)
                def _():
                    upward(k, below).start()

                sideways(k, below, m).start()

            @pl.when(above < span)
            def _():
                arrived(k, above * 4 + m * 2 + c)
                across(k, above).start()

                @pl.when(o > 0)
                def _():
                    downward(k, above).start()

                sideways(k, above, m).start()

    def across_wave(k):
        other = 1 - m
        arrived(k, o * 4 + other * 2 + c)
        sideways(k, o, other).start()
        for distance in range(1, span):
            below, above = o - distance, o + distance

            @pl.when(below >= 0)
            def _():
                arrived(k, below * 4 + other * 2 + c)
                sideways(k, below, other).start()

            @pl.when(above < span)
            def _():
                arrived(k, above * 4 + other * 2 + c)
                sideways(k, above, other).start()

    def side_wave(k):
        for line in range(span):
            for column in range(2):
                arrived(k, line * 4 + column * 2 + 1 - c)

    def chunk_rows(k):
        return gathered[k][:, :, 0:part].astype(F32).reshape(total, part).astype(BF16)

    def add_shrink(k, held):
        term = nt_dot(held, down_ref[:, k * part : (k + 1) * part])
        shrink[...] = term if k == 0 else shrink[...] + term

    def add_base(k, held):
        term = jnp.dot(held, w_ref[k * part : (k + 1) * part, :], preferred_element_type=F32)
        base[...] = term if k == 0 else base[...] + term

    def multiply(k):
        w_copy(k).wait()
        if k == 0:
            down_copy.wait()
        held = chunk_rows(k)
        add_shrink(k, held)
        if k < CHUNKS - 1:
            add_base(k, held)

    def pool_send_copy(d):
        return pltpu.make_async_remote_copy(
            src_ref=pool_hbm,
            dst_ref=own_pages,
            send_sem=pool_send.at[d],
            recv_sem=pool_recv.at[dec],
            device_id={"dec": lax.rem(dec + d, n_dec)},
            device_id_type=MESH,
        )

    def pool_arrived(owner):
        pltpu.make_async_remote_copy(
            src_ref=pool_hbm,
            dst_ref=pages.at[pl.ds(owner * pool_local, pool_local)],
            send_sem=pool_send.at[1],
            recv_sem=pool_recv.at[owner],
            device_id={"dec": lax.rem(dec + 1, n_dec)},
            device_id_type=MESH,
        ).wait_recv()

    send_own(0)
    for d in range(1, n_dec):
        pool_send_copy(d).start()
    send_own(1)
    for s in range(CHUNKS + 2):
        if s < CHUNKS:
            line_wave(s)
            if s + 2 < CHUNKS:
                send_own(s + 2)
        if 1 <= s <= CHUNKS:
            across_wave(s - 1)
        if s >= 2:
            side_wave(s - 2)
            multiply(s - 2)

    id_col = (
        gathered[0][:, :, part : part + LANES]
        .astype(F32)
        .reshape(total, LANES)[:, 0:1]
    )
    at_row, at_lane = iota((total, total), 0), iota((total, total), 1)
    id_row = jnp.sum(jnp.where(at_row == at_lane, id_col, 0.0), axis=0, keepdims=True)
    same = id_col == id_row
    row_rank = at_row // block * rows + at_row % rows
    lane_rank = at_lane // block * rows + at_lane % rows
    count_col = jnp.sum(
        jnp.where(same & (lane_rank < row_rank) & (at_lane % block < rows), 1.0, 0.0),
        axis=1,
        keepdims=True,
    )
    count_row = jnp.sum(
        jnp.where(same & (row_rank < lane_rank) & (at_row % block < rows), 1.0, 0.0),
        axis=0,
        keepdims=True,
    )
    slot, lane = iota((slots, total), 0), iota((slots, total), 1)
    pick = jnp.where(
        (slot // CAP == lane % block // rows)
        & (id_row == ada.astype(F32))
        & (count_row == (slot % CAP).astype(F32)),
        1.0,
        0.0,
    ).astype(BF16)
    row, place = iota((total, n * slots), 0), iota((total, n * slots), 1)
    spread = jnp.where(
        (row % block // rows == place % slots // CAP)
        & (id_col == (place // slots).astype(F32))
        & (count_col == (place % CAP).astype(F32)),
        1.0,
        0.0,
    ).astype(BF16)

    chosen = jnp.dot(pick, shrink[...].astype(BF16), preferred_element_type=F32).astype(BF16)
    up_copy.wait()

    def delta_of(target):
        columns = pl.ds(pl.multiple_of(target * head_cols, head_cols), head_cols)
        return jnp.dot(chosen, up_ref[:, columns], preferred_element_type=F32).astype(BF16)

    def d_copy(target):
        return pltpu.make_async_remote_copy(
            src_ref=d_send.at[target],
            dst_ref=d_recv.at[ada],
            send_sem=ds_sem.at[target],
            recv_sem=dr_sem.at[ada],
            device_id={"ada": target},
            device_id_type=MESH,
        )

    def d_arrived(source):
        pltpu.make_async_remote_copy(
            src_ref=d_send.at[source],
            dst_ref=d_recv.at[source],
            send_sem=ds_sem.at[source],
            recv_sem=dr_sem.at[source],
            device_id={"ada": source},
            device_id_type=MESH,
        ).wait_recv()

    order = sorted(range(1, n), key=lambda d: (abs(d - n // 2), d))
    targets = [lax.rem(ada + d, n) for d in order]
    sources = [lax.rem(ada + n - d, n) for d in order]
    for i, target in enumerate(targets):
        d_send[target] = delta_of(target)
        if i > 0:
            d_copy(targets[i - 1]).start()
    d_recv[ada] = delta_of(ada)
    d_copy(targets[-1]).start()

    add_base(CHUNKS - 1, chunk_rows(CHUNKS - 1))

    pool_copy.wait()
    for d in range(1, n_dec):
        pool_arrived(lax.rem(dec + d, n_dec))
    entries, page = table_ref.shape[1], pages.shape[2]
    cached = rows * entries * page
    for r in range(rows):
        for j in range(entries):
            held = pages[table_ref[r, j]]
            first = (r * entries + j) * page
            keys[first : first + page, :] = held[0]
            values[first : first + page, :] = held[1]
    fresh = [new_ref[u, r].astype(F32) for u in range(steps) for r in range(rows)]
    empty = jnp.zeros((keys.shape[0] - cached - block, keys.shape[1]), F32)
    keys[cached:, :] = jnp.concatenate([f[0:1] for f in fresh] + [empty], axis=0).astype(BF16)
    values[cached:, :] = jnp.concatenate([f[1:2] for f in fresh] + [empty], axis=0).astype(BF16)

    for source in sources:
        d_arrived(source)
    update = jnp.dot(
        spread, d_recv[...].reshape(n * slots, head_cols), preferred_element_type=F32
    )
    q_send[...] = (base[...] + update).reshape(n, block, head_cols).astype(BF16)
    q_recv[ada] = q_send[ada]

    def q_copy(target):
        return pltpu.make_async_remote_copy(
            src_ref=q_send.at[target],
            dst_ref=q_recv.at[ada],
            send_sem=qs_sem.at[target],
            recv_sem=qr_sem.at[ada],
            device_id={"ada": target},
            device_id_type=MESH,
        )

    def q_arrived(source):
        pltpu.make_async_remote_copy(
            src_ref=q_send.at[source],
            dst_ref=q_recv.at[source],
            send_sem=qs_sem.at[source],
            recv_sem=qr_sem.at[source],
            device_id={"ada": source},
            device_id_type=MESH,
        ).wait_recv()

    for target in targets:
        q_copy(target).start()

    kv_heads = keys.shape[1] // HD
    heads = width // HD
    group = heads // kv_heads
    count = keys.shape[0]
    query_at, key_at = iota((group * block, count), 0), iota((group * block, count), 1)
    query_step, query_row = query_at % block // rows, query_at % rows
    limit = jnp.zeros((group * block, count), jnp.int32)
    for r in range(rows):
        limit = jnp.where(query_row == r, len_ref[r], limit)
    in_cache = (
        (key_at < cached)
        & (key_at // (entries * page) == query_row)
        & (key_at % (entries * page) < limit)
    )
    late = key_at - cached
    in_new = (late >= 0) & (late % rows == query_row) & (late // rows <= query_step)
    allowed = in_cache | in_new
    scale = 1.0 / math.sqrt(HD)

    for source in sources:
        q_arrived(source)
    per_source = head_cols // HD
    for h in range(kv_heads):
        parts = []
        for g in range(group):
            head = h * group + g
            first = head % per_source * HD
            parts.append(q_recv[head // per_source, :, first : first + HD].astype(F32))
        query = jnp.concatenate(parts, axis=0).astype(BF16)
        lanes = slice(h * HD, (h + 1) * HD)
        scores = jnp.where(allowed, nt_dot(query, keys[:, lanes]) * scale, NEGATIVE)
        top = jnp.max(scores, axis=1, keepdims=True)
        weights = jnp.where(allowed, jnp.exp(scores - top), 0.0)
        denominator = jnp.sum(weights, axis=1, keepdims=True)
        high = weights.astype(BF16)
        low = (weights - high.astype(F32)).astype(BF16)
        both = jnp.dot(
            jnp.concatenate([high, low], axis=0), values[:, lanes], preferred_element_type=F32
        )
        attended = (both[: group * block] + both[group * block :]) / denominator
        for g in range(group):
            first = (h * group + g) * HD
            out_ref[:, first : first + HD] = attended[g * block : (g + 1) * block].astype(BF16)

    for k in range(CHUNKS):
        for line in range(span):
            across(k, line).wait_send()

            @pl.when((line <= o) & (o < span - 1))
            def _():
                upward(k, line).wait_send()

            @pl.when((line >= o) & (o > 0))
            def _():
                downward(k, line).wait_send()

            for column in range(2):
                sideways(k, line, column).wait_send()
    for d in range(1, n_dec):
        pool_send_copy(d).wait_send()
    for target in targets:
        d_copy(target).wait_send()
        q_copy(target).wait_send()


def body(
    inputs,
    query_weight,
    adapter_down,
    adapter_up,
    adapter_ids,
    new_cache,
    cache_pool,
    page_table,
    lengths,
):
    n, n_dec = lax.axis_size("ada"), lax.axis_size("dec")
    steps, rows, width = inputs.shape
    held, _, rank = adapter_down.shape
    assert held == 1 and n % 4 == 0
    head_cols = query_weight.shape[1]
    block, slots, span = steps * rows, steps * CAP, n // 4
    part = width // CHUNKS
    pool_local, _, page, kv_width = cache_pool.shape
    count = -(-(rows * page_table.shape[1] * page + block) // 16) * 16
    dma = pltpu.SemaphoreType.DMA
    vmem, smem, hbm = (
        pl.BlockSpec(memory_space=pltpu.VMEM),
        pl.BlockSpec(memory_space=pltpu.SMEM),
        pl.BlockSpec(memory_space=pl.ANY),
    )
    scratch = [
        pltpu.VMEM((n, block, part + (LANES if k == 0 else 0)), BF16) for k in range(CHUNKS)
    ] + [
        pltpu.VMEM((width, head_cols), BF16),
        pltpu.VMEM((rank, width), BF16),
        pltpu.VMEM((rank, width), BF16),
        pltpu.VMEM((n_dec * pool_local, 2, page, kv_width), BF16),
        pltpu.VMEM((n * block, head_cols), F32),
        pltpu.VMEM((n * block, rank), F32),
        pltpu.VMEM((n, slots, head_cols), BF16),
        pltpu.VMEM((n, slots, head_cols), BF16),
        pltpu.VMEM((n, block, head_cols), BF16),
        pltpu.VMEM((n, block, head_cols), BF16),
        pltpu.VMEM((count, kv_width), BF16),
        pltpu.VMEM((count, kv_width), BF16),
        dma((CHUNKS,)),
        dma,
        dma,
        dma,
        dma((n_dec,)),
        dma((n_dec,)),
        dma((CHUNKS, span)),
        dma((CHUNKS, span)),
        dma((CHUNKS, span)),
        dma((CHUNKS, 2 * span)),
        dma((CHUNKS, n)),
        dma((n,)),
        dma((n,)),
        dma((n,)),
        dma((n,)),
    ]
    out = pl.pallas_call(
        functools.partial(kernel, n, n_dec),
        out_shape=jax.ShapeDtypeStruct((block, width), BF16),
        in_specs=[vmem, hbm, hbm, hbm, smem, vmem, hbm, smem, smem],
        out_specs=vmem,
        scratch_shapes=scratch,
        compiler_params=pltpu.CompilerParams(
            collective_id=0, has_side_effects=True, vmem_limit_bytes=60 * 1024 * 1024
        ),
    )(
        inputs,
        query_weight,
        jnp.swapaxes(adapter_down[0], 0, 1),
        adapter_up[0],
        adapter_ids[:, 0],
        new_cache,
        cache_pool,
        page_table,
        lengths,
    )
    return out.reshape(steps, rows, width)


def solution(mesh):
    in_specs = (
        P(None, ("dec", "ada"), None),
        P(None, "ada"),
        P(("dec", "ada"), None, None),
        P(("dec", "ada"), None, None),
        P(("dec", "ada"), None),
        P(None, ("dec", "ada"), None, None),
        P(("dec", "ada"), None, None, None),
        P(("dec", "ada"), None),
        P(("dec", "ada")),
    )
    out_specs = P(None, ("dec", "ada"), None)
    return jax.shard_map(body, mesh=mesh, in_specs=in_specs, out_specs=out_specs, check_vma=False)
```

```python
import functools
import math

import jax
import jax.numpy as jnp
from jax import lax
from jax.experimental import pallas as pl
from jax.experimental.pallas import tpu as pltpu
from jax.sharding import PartitionSpec as P

HD = 128
CAP = 4
LANES = 128
CHUNKS = 2
AHEAD = 2
REACH = 2
NEGATIVE = -1e30
MESH = pl.DeviceIdType.MESH
F32 = jnp.float32
BF16 = jnp.bfloat16


def nt_dot(a, b):
    return lax.dot_general(a, b, (((1,), (1,)), ((), ())), preferred_element_type=F32)


def iota(shape, axis):
    return lax.broadcasted_iota(jnp.int32, shape, axis)


def kernel(
    n,
    n_dec,
    x_ref,
    w_hbm,
    down_hbm,
    up_hbm,
    ids_ref,
    new_ref,
    pool_hbm,
    table_ref,
    len_ref,
    out_ref,
    *scratch,
):
    gathered = scratch[:CHUNKS]
    (
        w_ref, down_ref, up_ref, pages, base, shrink, d_send, d_recv, q_send, q_recv, keys, values, result,
        w_sem, down_sem, up_sem, pool_sem, pool_send, pool_recv,
        up_send, low_send, across_send, side_send, g_recv, ds_sem, dr_sem, qs_sem, qr_sem,
    ) = scratch[CHUNKS:]
    ada, dec = lax.axis_index("ada"), lax.axis_index("dec")
    steps, rows, width = x_ref.shape
    part = width // CHUNKS
    block = steps * rows
    total = n * block
    head_cols = w_ref.shape[1]
    slots = steps * CAP
    span = n // 4
    o, m, c = ada // 4, (ada // 2) % 2, ada % 2
    sibling = ada + 1 - 2 * c
    opposite = ada + 2 - 4 * m
    pool_local = pool_hbm.shape[0]

    def w_copy(k):
        where = pl.ds(k * part, part)
        return pltpu.make_async_copy(w_hbm.at[where], w_ref.at[where], w_sem.at[k])

    down_copy = pltpu.make_async_copy(down_hbm, down_ref, down_sem)
    up_copy = pltpu.make_async_copy(up_hbm, up_ref, up_sem)
    own_pages = pages.at[pl.ds(dec * pool_local, pool_local)]
    pool_copy = pltpu.make_async_copy(pool_hbm, own_pages, pool_sem)

    mine = jnp.concatenate([x_ref[t].astype(F32) for t in range(steps)], axis=0).astype(BF16)
    row_of = iota((block, LANES), 0) % rows
    id_block = jnp.zeros((block, LANES), F32)
    for r in range(rows):
        id_block = jnp.where(row_of == r, ids_ref[r].astype(F32), id_block)
    for k in range(CHUNKS):
        gathered[k][ada, :, 0:part] = mine[:, k * part : (k + 1) * part]
    gathered[0][ada, :, part : part + LANES] = id_block.astype(BF16)

    barrier = pltpu.get_barrier_semaphore()

    def greet(peer):
        pl.semaphore_signal(barrier, inc=1, device_id={"ada": peer}, device_id_type=MESH)

    greet(opposite)
    greet(sibling)
    for distance in range(1, min(REACH, span - 1) + 1):
        for side in (1, -1):

            @pl.when((o + side * distance >= 0) & (o + side * distance < span))
            def _():
                greet(ada + 4 * side * distance)

    line_peers = 0
    for distance in range(1, min(REACH, span - 1) + 1):
        line_peers += (o >= distance).astype(jnp.int32) + (o + distance < span).astype(jnp.int32)
    for d in range(1, n_dec):
        pl.semaphore_signal(
            barrier, inc=1, device_id={"dec": lax.rem(dec + d, n_dec)}, device_id_type=MESH
        )
    w_copy(0).start()
    down_copy.start()
    for k in range(1, CHUNKS):
        w_copy(k).start()
    up_copy.start()
    pool_copy.start()
    pl.semaphore_wait(barrier, line_peers + 2 + n_dec - 1)

    def relay(k, source, send_sem, peer):
        return pltpu.make_async_remote_copy(
            src_ref=gathered[k].at[source],
            dst_ref=gathered[k].at[source],
            send_sem=send_sem,
            recv_sem=g_recv.at[k, source],
            device_id={"ada": peer},
            device_id_type=MESH,
        )

    def arrived(k, source):
        relay(k, source, side_send.at[k, 0], sibling).wait_recv()

    def upward(k, line):
        return relay(k, line * 4 + m * 2 + c, up_send.at[k, line], ada + 4)

    def downward(k, line):
        return relay(k, line * 4 + m * 2 + c, low_send.at[k, line], ada - 4)

    def far_up(k):
        return relay(k, ada, up_send.at[k, span], ada + 8)

    def far_down(k):
        return relay(k, ada, low_send.at[k, span], ada - 8)

    def across(k, line):
        return relay(k, line * 4 + m * 2 + c, across_send.at[k, line], opposite)

    def sideways(k, line, column):
        return relay(
            k, line * 4 + column * 2 + c, side_send.at[k, line * 2 + column], sibling
        )

    def send_own(k):
        across(k, o).start()

        @pl.when(o < span - 1)
        def _():
            upward(k, o).start()

        @pl.when(o > 0)
        def _():
            downward(k, o).start()

        @pl.when(o < span - 2)
        def _():
            far_up(k).start()

        @pl.when(o > 1)
        def _():
            far_down(k).start()

        sideways(k, o, m).start()

    def line_event(k, distance):
        below, above = o - distance, o + distance

        @pl.when(below >= 0)
        def _():
            arrived(k, below * 4 + m * 2 + c)
            across(k, below).start()
            if distance >= REACH:

                @pl.when(o < span - 1)
                def _():
                    upward(k, below).start()

            sideways(k, below, m).start()

        @pl.when(above < span)
        def _():
            arrived(k, above * 4 + m * 2 + c)
            across(k, above).start()
            if distance >= REACH:

                @pl.when(o > 0)
                def _():
                    downward(k, above).start()

            sideways(k, above, m).start()

    def across_event(k, distance):
        other = 1 - m
        below, above = o - distance, o + distance

        @pl.when(below >= 0)
        def _():
            arrived(k, below * 4 + other * 2 + c)
            sideways(k, below, other).start()

        if distance:

            @pl.when(above < span)
            def _():
                arrived(k, above * 4 + other * 2 + c)
                sideways(k, above, other).start()

    def side_wave(k):
        for line in range(span):
            for column in range(2):
                arrived(k, line * 4 + column * 2 + 1 - c)

    def chunk_rows(k):
        return gathered[k][:, :, 0:part].astype(F32).reshape(total, part).astype(BF16)

    def add_shrink(k, held):
        term = nt_dot(held, down_ref[:, k * part : (k + 1) * part])
        shrink[...] = term if k == 0 else shrink[...] + term

    def add_base(k, held):
        term = jnp.dot(held, w_ref[k * part : (k + 1) * part, :], preferred_element_type=F32)
        base[...] = term if k == 0 else base[...] + term

    def multiply(k):
        w_copy(k).wait()
        if k == 0:
            down_copy.wait()
        held = chunk_rows(k)
        add_shrink(k, held)
        if k < CHUNKS - 1:
            add_base(k, held)

    def pool_send_copy(d):
        return pltpu.make_async_remote_copy(
            src_ref=pool_hbm,
            dst_ref=own_pages,
            send_sem=pool_send.at[d],
            recv_sem=pool_recv.at[dec],
            device_id={"dec": lax.rem(dec + d, n_dec)},
            device_id_type=MESH,
        )

    def pool_arrived(owner):
        pltpu.make_async_remote_copy(
            src_ref=pool_hbm,
            dst_ref=pages.at[pl.ds(owner * pool_local, pool_local)],
            send_sem=pool_send.at[1],
            recv_sem=pool_recv.at[owner],
            device_id={"dec": lax.rem(dec + 1, n_dec)},
            device_id_type=MESH,
        ).wait_recv()

    def slot_masks():
        id_col = (
            gathered[0][:, :, part : part + LANES]
            .astype(F32)
            .reshape(total, LANES)[:, 0:1]
        )
        at_row, at_lane = iota((total, total), 0), iota((total, total), 1)
        id_row = jnp.sum(jnp.where(at_row == at_lane, id_col, 0.0), axis=0, keepdims=True)
        same = id_col == id_row
        row_rank = at_row // block * rows + at_row % rows
        lane_rank = at_lane // block * rows + at_lane % rows
        count_col = jnp.sum(
            jnp.where(same & (lane_rank < row_rank) & (at_lane % block < rows), 1.0, 0.0),
            axis=1,
            keepdims=True,
        )
        count_row = jnp.sum(
            jnp.where(same & (row_rank < lane_rank) & (at_row % block < rows), 1.0, 0.0),
            axis=0,
            keepdims=True,
        )
        slot, lane = iota((slots, total), 0), iota((slots, total), 1)
        pick = jnp.where(
            (slot // CAP == lane % block // rows)
            & (id_row == ada.astype(F32))
            & (count_row == (slot % CAP).astype(F32)),
            1.0,
            0.0,
        ).astype(BF16)
        row, place = iota((total, n * slots), 0), iota((total, n * slots), 1)
        spread = jnp.where(
            (row % block // rows == place % slots // CAP)
            & (id_col == (place // slots).astype(F32))
            & (count_col == (place % CAP).astype(F32)),
            1.0,
            0.0,
        ).astype(BF16)
        return pick, spread

    entries, page = table_ref.shape[1], pages.shape[2]
    cached = rows * entries * page
    kv_heads = keys.shape[1] // HD
    heads = width // HD
    group = heads // kv_heads
    count = keys.shape[0]

    def key_mask():
        query_at, key_at = iota((group * block, count), 0), iota((group * block, count), 1)
        query_step, query_row = query_at % block // rows, query_at % rows
        limit = jnp.zeros((group * block, count), jnp.int32)
        for r in range(rows):
            limit = jnp.where(query_row == r, len_ref[r], limit)
        in_cache = (
            (key_at < cached)
            & (key_at // (entries * page) == query_row)
            & (key_at % (entries * page) < limit)
        )
        late = key_at - cached
        in_new = (late >= 0) & (late % rows == query_row) & (late // rows <= query_step)
        return in_cache | in_new

    for k in range(min(AHEAD, CHUNKS)):
        send_own(k)
        if k == 0:
            for d in range(1, n_dec):
                pool_send_copy(d).start()
    lag = max(0, span - 1 - REACH)
    pick = spread = allowed = id_col = None
    for tick in range(CHUNKS + lag + 2):
        for distance in range(1, span):
            k = tick - max(0, distance - REACH)
            if 0 <= k < CHUNKS:
                line_event(k, distance)
        if tick + AHEAD < CHUNKS:
            send_own(tick + AHEAD)
        for distance in range(span):
            k = tick - 1 - max(0, distance - REACH)
            if 0 <= k < CHUNKS:
                across_event(k, distance)
        k = tick - lag - 2
        if 0 <= k < CHUNKS:
            side_wave(k)
            multiply(k)
            if k == 0:
                pick, spread = slot_masks()
            if k == min(1, CHUNKS - 1):
                allowed = key_mask()

    chosen = jnp.dot(pick, shrink[...].astype(BF16), preferred_element_type=F32).astype(BF16)
    up_copy.wait()

    def delta_of(target):
        columns = pl.ds(pl.multiple_of(target * head_cols, head_cols), head_cols)
        return jnp.dot(chosen, up_ref[:, columns], preferred_element_type=F32).astype(BF16)

    def d_copy(target):
        return pltpu.make_async_remote_copy(
            src_ref=d_send.at[target],
            dst_ref=d_recv.at[ada],
            send_sem=ds_sem.at[target],
            recv_sem=dr_sem.at[ada],
            device_id={"ada": target},
            device_id_type=MESH,
        )

    def d_arrived(source):
        pltpu.make_async_remote_copy(
            src_ref=d_send.at[source],
            dst_ref=d_recv.at[source],
            send_sem=ds_sem.at[source],
            recv_sem=dr_sem.at[source],
            device_id={"ada": source},
            device_id_type=MESH,
        ).wait_recv()

    order = sorted(range(1, n), key=lambda d: (abs(d - n // 2), d))
    targets = [lax.rem(ada + d, n) for d in order]
    sources = [lax.rem(ada + n - d, n) for d in order]
    for i, target in enumerate(targets):
        d_send[target] = delta_of(target)
        if i > 0:
            d_copy(targets[i - 1]).start()
    d_recv[ada] = delta_of(ada)
    d_copy(targets[-1]).start()

    add_base(CHUNKS - 1, chunk_rows(CHUNKS - 1))

    pool_copy.wait()
    for d in range(1, n_dec):
        pool_arrived(lax.rem(dec + d, n_dec))
    for r in range(rows):
        for j in range(entries):
            held = pages[table_ref[r, j]]
            first = (r * entries + j) * page
            keys[first : first + page, :] = held[0]
            values[first : first + page, :] = held[1]
    fresh = [new_ref[u, r].astype(F32) for u in range(steps) for r in range(rows)]
    empty = jnp.zeros((keys.shape[0] - cached - block, keys.shape[1]), F32)
    keys[cached:, :] = jnp.concatenate([f[0:1] for f in fresh] + [empty], axis=0).astype(BF16)
    values[cached:, :] = jnp.concatenate([f[1:2] for f in fresh] + [empty], axis=0).astype(BF16)

    for source in sources:
        d_arrived(source)
    update = jnp.dot(
        spread, d_recv[...].reshape(n * slots, head_cols), preferred_element_type=F32
    )
    q_send[...] = (base[...] + update).reshape(n, block, head_cols).astype(BF16)
    q_recv[ada] = q_send[ada]

    def q_copy(target):
        return pltpu.make_async_remote_copy(
            src_ref=q_send.at[target],
            dst_ref=q_recv.at[ada],
            send_sem=qs_sem.at[target],
            recv_sem=qr_sem.at[ada],
            device_id={"ada": target},
            device_id_type=MESH,
        )

    def q_arrived(source):
        pltpu.make_async_remote_copy(
            src_ref=q_send.at[source],
            dst_ref=q_recv.at[source],
            send_sem=qs_sem.at[source],
            recv_sem=qr_sem.at[source],
            device_id={"ada": source},
            device_id_type=MESH,
        ).wait_recv()

    for target in targets:
        q_copy(target).start()

    scale = 1.0 / math.sqrt(HD)

    for source in sources:
        q_arrived(source)
    per_source = head_cols // HD
    for h in range(kv_heads):
        parts = []
        for g in range(group):
            head = h * group + g
            first = head % per_source * HD
            parts.append(q_recv[head // per_source, :, first : first + HD].astype(F32))
        query = jnp.concatenate(parts, axis=0).astype(BF16)
        lanes = slice(h * HD, (h + 1) * HD)
        scores = jnp.where(allowed, nt_dot(query, keys[:, lanes]) * scale, NEGATIVE)
        top = jnp.max(scores, axis=1, keepdims=True)
        weights = jnp.where(allowed, jnp.exp(scores - top), 0.0)
        denominator = jnp.sum(weights, axis=1, keepdims=True)
        high = weights.astype(BF16)
        low = (weights - high.astype(F32)).astype(BF16)
        both = jnp.dot(
            jnp.concatenate([high, low], axis=0), values[:, lanes], preferred_element_type=F32
        )
        attended = (both[: group * block] + both[group * block :]) / denominator
        for g in range(group):
            first = (h * group + g) * HD
            result[:, first : first + HD] = attended[g * block : (g + 1) * block]

    for t in range(steps):
        out_ref[t] = result[t * rows : (t + 1) * rows, :].astype(BF16)

    for k in range(CHUNKS):

        @pl.when(o < span - 2)
        def _():
            far_up(k).wait_send()

        @pl.when(o > 1)
        def _():
            far_down(k).wait_send()

        for line in range(span):
            across(k, line).wait_send()

            @pl.when(((line == o) | (line <= o - REACH)) & (o < span - 1))
            def _():
                upward(k, line).wait_send()

            @pl.when(((line == o) | (line >= o + REACH)) & (o > 0))
            def _():
                downward(k, line).wait_send()

            for column in range(2):
                sideways(k, line, column).wait_send()
    for d in range(1, n_dec):
        pool_send_copy(d).wait_send()
    for target in targets:
        d_copy(target).wait_send()
        q_copy(target).wait_send()


def body(
    inputs,
    query_weight,
    adapter_down,
    adapter_up,
    adapter_ids,
    new_cache,
    cache_pool,
    page_table,
    lengths,
):
    n, n_dec = lax.axis_size("ada"), lax.axis_size("dec")
    steps, rows, width = inputs.shape
    held, _, rank = adapter_down.shape
    assert held == 1 and n % 4 == 0
    head_cols = query_weight.shape[1]
    block, slots, span = steps * rows, steps * CAP, n // 4
    part = width // CHUNKS
    pool_local, _, page, kv_width = cache_pool.shape
    count = -(-(rows * page_table.shape[1] * page + block) // 16) * 16
    dma = pltpu.SemaphoreType.DMA
    vmem, smem, hbm = (
        pl.BlockSpec(memory_space=pltpu.VMEM),
        pl.BlockSpec(memory_space=pltpu.SMEM),
        pl.BlockSpec(memory_space=pl.ANY),
    )
    scratch = [
        pltpu.VMEM((n, block, part + (LANES if k == 0 else 0)), BF16) for k in range(CHUNKS)
    ] + [
        pltpu.VMEM((width, head_cols), BF16),
        pltpu.VMEM((rank, width), BF16),
        pltpu.VMEM((rank, width), BF16),
        pltpu.VMEM((n_dec * pool_local, 2, page, kv_width), BF16),
        pltpu.VMEM((n * block, head_cols), F32),
        pltpu.VMEM((n * block, rank), F32),
        pltpu.VMEM((n, slots, head_cols), BF16),
        pltpu.VMEM((n, slots, head_cols), BF16),
        pltpu.VMEM((n, block, head_cols), BF16),
        pltpu.VMEM((n, block, head_cols), BF16),
        pltpu.VMEM((count, kv_width), BF16),
        pltpu.VMEM((count, kv_width), BF16),
        pltpu.VMEM((block, width), F32),
        dma((CHUNKS,)),
        dma,
        dma,
        dma,
        dma((n_dec,)),
        dma((n_dec,)),
        dma((CHUNKS, span + 1)),
        dma((CHUNKS, span + 1)),
        dma((CHUNKS, span)),
        dma((CHUNKS, 2 * span)),
        dma((CHUNKS, n)),
        dma((n,)),
        dma((n,)),
        dma((n,)),
        dma((n,)),
    ]
    return pl.pallas_call(
        functools.partial(kernel, n, n_dec),
        out_shape=jax.ShapeDtypeStruct((steps, rows, width), BF16),
        in_specs=[vmem, hbm, hbm, hbm, smem, vmem, hbm, smem, smem],
        out_specs=vmem,
        scratch_shapes=scratch,
        compiler_params=pltpu.CompilerParams(
            collective_id=0, has_side_effects=True, vmem_limit_bytes=60 * 1024 * 1024
        ),
    )(
        inputs,
        query_weight,
        jnp.swapaxes(adapter_down[0], 0, 1),
        adapter_up[0],
        adapter_ids[:, 0],
        new_cache,
        cache_pool,
        page_table,
        lengths,
    )


def solution(mesh):
    in_specs = (
        P(None, ("dec", "ada"), None),
        P(None, "ada"),
        P(("dec", "ada"), None, None),
        P(("dec", "ada"), None, None),
        P(("dec", "ada"), None),
        P(None, ("dec", "ada"), None, None),
        P(("dec", "ada"), None, None, None),
        P(("dec", "ada"), None),
        P(("dec", "ada")),
    )
    out_specs = P(None, ("dec", "ada"), None)
    return jax.shard_map(body, mesh=mesh, in_specs=in_specs, out_specs=out_specs, check_vma=False)
```

```python
import functools
import math

import jax
import jax.numpy as jnp
from jax import lax
from jax.experimental import pallas as pl
from jax.experimental.pallas import tpu as pltpu
from jax.sharding import PartitionSpec as P

HD = 128
CAP = 4
LANES = 128
CHUNKS = 2
EDGES = (0, 10, 16)
AHEAD = 2
REACH = 2
NEGATIVE = -1e30
MESH = pl.DeviceIdType.MESH
F32 = jnp.float32
BF16 = jnp.bfloat16


def nt_dot(a, b):
    return lax.dot_general(a, b, (((1,), (1,)), ((), ())), preferred_element_type=F32)


def iota(shape, axis):
    return lax.broadcasted_iota(jnp.int32, shape, axis)


def kernel(
    n,
    n_dec,
    x_ref,
    w_hbm,
    down_hbm,
    up_hbm,
    ids_ref,
    new_ref,
    pool_hbm,
    table_ref,
    len_ref,
    out_ref,
    *scratch,
):
    gathered = scratch[:CHUNKS]
    (
        w_ref, down_ref, up_ref, pages, base, shrink, d_send, d_recv, q_send, q_recv, keys, values, result,
        w_sem, down_sem, up_sem, pool_sem, pool_send, pool_recv,
        up_send, low_send, across_send, side_send, g_recv, ds_sem, dr_sem, qs_sem, qr_sem,
    ) = scratch[CHUNKS:]
    ada, dec = lax.axis_index("ada"), lax.axis_index("dec")
    steps, rows, width = x_ref.shape
    edges = [width // EDGES[-1] * e for e in EDGES]
    sizes = [b - a for a, b in zip(edges[:-1], edges[1:])]
    part = sizes[0]
    block = steps * rows
    total = n * block
    head_cols = w_ref.shape[1]
    slots = steps * CAP
    span = n // 4
    o, m, c = ada // 4, (ada // 2) % 2, ada % 2
    sibling = ada + 1 - 2 * c
    opposite = ada + 2 - 4 * m
    pool_local = pool_hbm.shape[0]

    def w_copy(k):
        where = pl.ds(edges[k], sizes[k])
        return pltpu.make_async_copy(w_hbm.at[where], w_ref.at[where], w_sem.at[k])

    down_copy = pltpu.make_async_copy(down_hbm, down_ref, down_sem)
    up_copy = pltpu.make_async_copy(up_hbm, up_ref, up_sem)
    own_pages = pages.at[pl.ds(dec * pool_local, pool_local)]
    pool_copy = pltpu.make_async_copy(pool_hbm, own_pages, pool_sem)

    mine = jnp.concatenate([x_ref[t].astype(F32) for t in range(steps)], axis=0).astype(BF16)
    row_of = iota((block, LANES), 0) % rows
    id_block = jnp.zeros((block, LANES), F32)
    for r in range(rows):
        id_block = jnp.where(row_of == r, ids_ref[r].astype(F32), id_block)
    for k in range(CHUNKS):
        gathered[k][ada, :, 0 : sizes[k]] = mine[:, edges[k] : edges[k + 1]]
    gathered[0][ada, :, part : part + LANES] = id_block.astype(BF16)

    barrier = pltpu.get_barrier_semaphore()

    def greet(peer):
        pl.semaphore_signal(barrier, inc=1, device_id={"ada": peer}, device_id_type=MESH)

    greet(opposite)
    greet(sibling)
    for distance in range(1, min(REACH, span - 1) + 1):
        for side in (1, -1):

            @pl.when((o + side * distance >= 0) & (o + side * distance < span))
            def _():
                greet(ada + 4 * side * distance)

    line_peers = 0
    for distance in range(1, min(REACH, span - 1) + 1):
        line_peers += (o >= distance).astype(jnp.int32) + (o + distance < span).astype(jnp.int32)
    for d in range(1, n_dec):
        pl.semaphore_signal(
            barrier, inc=1, device_id={"dec": lax.rem(dec + d, n_dec)}, device_id_type=MESH
        )
    w_copy(0).start()
    down_copy.start()
    for k in range(1, CHUNKS):
        w_copy(k).start()
    up_copy.start()
    pool_copy.start()
    pl.semaphore_wait(barrier, line_peers + 2 + n_dec - 1)

    def relay(k, source, send_sem, peer):
        return pltpu.make_async_remote_copy(
            src_ref=gathered[k].at[source],
            dst_ref=gathered[k].at[source],
            send_sem=send_sem,
            recv_sem=g_recv.at[k, source],
            device_id={"ada": peer},
            device_id_type=MESH,
        )

    def arrived(k, source):
        relay(k, source, side_send.at[k, 0], sibling).wait_recv()

    def upward(k, line):
        return relay(k, line * 4 + m * 2 + c, up_send.at[k, line], ada + 4)

    def downward(k, line):
        return relay(k, line * 4 + m * 2 + c, low_send.at[k, line], ada - 4)

    def far_up(k):
        return relay(k, ada, up_send.at[k, span], ada + 8)

    def far_down(k):
        return relay(k, ada, low_send.at[k, span], ada - 8)

    def across(k, line):
        return relay(k, line * 4 + m * 2 + c, across_send.at[k, line], opposite)

    def sideways(k, line, column):
        return relay(
            k, line * 4 + column * 2 + c, side_send.at[k, line * 2 + column], sibling
        )

    def send_own(k):
        across(k, o).start()

        @pl.when(o < span - 1)
        def _():
            upward(k, o).start()

        @pl.when(o > 0)
        def _():
            downward(k, o).start()

        @pl.when(o < span - 2)
        def _():
            far_up(k).start()

        @pl.when(o > 1)
        def _():
            far_down(k).start()

        sideways(k, o, m).start()

    def line_event(k, distance):
        below, above = o - distance, o + distance

        @pl.when(below >= 0)
        def _():
            arrived(k, below * 4 + m * 2 + c)
            across(k, below).start()
            if distance >= REACH:

                @pl.when(o < span - 1)
                def _():
                    upward(k, below).start()

            sideways(k, below, m).start()

        @pl.when(above < span)
        def _():
            arrived(k, above * 4 + m * 2 + c)
            across(k, above).start()
            if distance >= REACH:

                @pl.when(o > 0)
                def _():
                    downward(k, above).start()

            sideways(k, above, m).start()

    def across_event(k, distance):
        other = 1 - m
        below, above = o - distance, o + distance

        @pl.when(below >= 0)
        def _():
            arrived(k, below * 4 + other * 2 + c)
            sideways(k, below, other).start()

        if distance:

            @pl.when(above < span)
            def _():
                arrived(k, above * 4 + other * 2 + c)
                sideways(k, above, other).start()

    def side_wave(k):
        for line in range(span):
            for column in range(2):
                arrived(k, line * 4 + column * 2 + 1 - c)

    def chunk_rows(k):
        return gathered[k][:, :, 0 : sizes[k]].astype(F32).reshape(total, sizes[k]).astype(BF16)

    def add_shrink(k, held):
        term = nt_dot(held, down_ref[:, edges[k] : edges[k + 1]])
        shrink[...] = term if k == 0 else shrink[...] + term

    def add_base(k, held):
        term = jnp.dot(held, w_ref[edges[k] : edges[k + 1], :], preferred_element_type=F32)
        base[...] = term if k == 0 else base[...] + term

    def multiply(k):
        w_copy(k).wait()
        if k == 0:
            down_copy.wait()
        held = chunk_rows(k)
        add_shrink(k, held)
        if k < CHUNKS - 1:
            add_base(k, held)

    def pool_send_copy(d):
        return pltpu.make_async_remote_copy(
            src_ref=pool_hbm,
            dst_ref=own_pages,
            send_sem=pool_send.at[d],
            recv_sem=pool_recv.at[dec],
            device_id={"dec": lax.rem(dec + d, n_dec)},
            device_id_type=MESH,
        )

    def pool_arrived(owner):
        pltpu.make_async_remote_copy(
            src_ref=pool_hbm,
            dst_ref=pages.at[pl.ds(owner * pool_local, pool_local)],
            send_sem=pool_send.at[1],
            recv_sem=pool_recv.at[owner],
            device_id={"dec": lax.rem(dec + 1, n_dec)},
            device_id_type=MESH,
        ).wait_recv()

    def slot_masks():
        id_col = (
            gathered[0][:, :, part : part + LANES]
            .astype(F32)
            .reshape(total, LANES)[:, 0:1]
        )
        at_row, at_lane = iota((total, total), 0), iota((total, total), 1)
        id_row = jnp.sum(jnp.where(at_row == at_lane, id_col, 0.0), axis=0, keepdims=True)
        same = id_col == id_row
        row_rank = at_row // block * rows + at_row % rows
        lane_rank = at_lane // block * rows + at_lane % rows
        count_col = jnp.sum(
            jnp.where(same & (lane_rank < row_rank) & (at_lane % block < rows), 1.0, 0.0),
            axis=1,
            keepdims=True,
        )
        count_row = jnp.sum(
            jnp.where(same & (row_rank < lane_rank) & (at_row % block < rows), 1.0, 0.0),
            axis=0,
            keepdims=True,
        )
        slot, lane = iota((slots, total), 0), iota((slots, total), 1)
        pick = jnp.where(
            (slot // CAP == lane % block // rows)
            & (id_row == ada.astype(F32))
            & (count_row == (slot % CAP).astype(F32)),
            1.0,
            0.0,
        ).astype(BF16)
        row, place = iota((total, n * slots), 0), iota((total, n * slots), 1)
        spread = jnp.where(
            (row % block // rows == place % slots // CAP)
            & (id_col == (place // slots).astype(F32))
            & (count_col == (place % CAP).astype(F32)),
            1.0,
            0.0,
        ).astype(BF16)
        return pick, spread

    entries, page = table_ref.shape[1], pages.shape[2]
    cached = rows * entries * page
    kv_heads = keys.shape[1] // HD
    heads = width // HD
    group = heads // kv_heads
    count = keys.shape[0]

    def key_mask():
        query_at, key_at = iota((group * block, count), 0), iota((group * block, count), 1)
        query_step, query_row = query_at % block // rows, query_at % rows
        limit = jnp.zeros((group * block, count), jnp.int32)
        for r in range(rows):
            limit = jnp.where(query_row == r, len_ref[r], limit)
        in_cache = (
            (key_at < cached)
            & (key_at // (entries * page) == query_row)
            & (key_at % (entries * page) < limit)
        )
        late = key_at - cached
        in_new = (late >= 0) & (late % rows == query_row) & (late // rows <= query_step)
        return in_cache | in_new

    for k in range(min(AHEAD, CHUNKS)):
        send_own(k)
        if k == 0:
            for d in range(1, n_dec):
                pool_send_copy(d).start()
    lag = max(0, span - 1 - REACH)
    pick = spread = allowed = id_col = None
    for tick in range(CHUNKS + lag + 2):
        for distance in range(1, span):
            k = tick - max(0, distance - REACH)
            if 0 <= k < CHUNKS:
                line_event(k, distance)
        if tick + AHEAD < CHUNKS:
            send_own(tick + AHEAD)
        for distance in range(span):
            k = tick - 1 - max(0, distance - REACH)
            if 0 <= k < CHUNKS:
                across_event(k, distance)
        k = tick - lag - 2
        if 0 <= k < CHUNKS:
            side_wave(k)
            multiply(k)
            if k == 0:
                pick, spread = slot_masks()
            if k == min(1, CHUNKS - 1):
                allowed = key_mask()

    chosen = jnp.dot(pick, shrink[...].astype(BF16), preferred_element_type=F32).astype(BF16)
    up_copy.wait()

    def delta_of(target):
        columns = pl.ds(pl.multiple_of(target * head_cols, head_cols), head_cols)
        return jnp.dot(chosen, up_ref[:, columns], preferred_element_type=F32).astype(BF16)

    def d_copy(target):
        return pltpu.make_async_remote_copy(
            src_ref=d_send.at[target],
            dst_ref=d_recv.at[ada],
            send_sem=ds_sem.at[target],
            recv_sem=dr_sem.at[ada],
            device_id={"ada": target},
            device_id_type=MESH,
        )

    def d_arrived(source):
        pltpu.make_async_remote_copy(
            src_ref=d_send.at[source],
            dst_ref=d_recv.at[source],
            send_sem=ds_sem.at[source],
            recv_sem=dr_sem.at[source],
            device_id={"ada": source},
            device_id_type=MESH,
        ).wait_recv()

    order = sorted(range(1, n), key=lambda d: (abs(d - n // 2), d))
    targets = [lax.rem(ada + d, n) for d in order]
    sources = [lax.rem(ada + n - d, n) for d in order]
    for i, target in enumerate(targets):
        d_send[target] = delta_of(target)
        if i > 0:
            d_copy(targets[i - 1]).start()
    d_recv[ada] = delta_of(ada)
    d_copy(targets[-1]).start()

    add_base(CHUNKS - 1, chunk_rows(CHUNKS - 1))

    pool_copy.wait()
    for d in range(1, n_dec):
        pool_arrived(lax.rem(dec + d, n_dec))
    for r in range(rows):
        for j in range(entries):
            held = pages[table_ref[r, j]]
            first = (r * entries + j) * page
            keys[first : first + page, :] = held[0]
            values[first : first + page, :] = held[1]
    fresh = [new_ref[u, r].astype(F32) for u in range(steps) for r in range(rows)]
    empty = jnp.zeros((keys.shape[0] - cached - block, keys.shape[1]), F32)
    keys[cached:, :] = jnp.concatenate([f[0:1] for f in fresh] + [empty], axis=0).astype(BF16)
    values[cached:, :] = jnp.concatenate([f[1:2] for f in fresh] + [empty], axis=0).astype(BF16)

    for source in sources:
        d_arrived(source)
    update = jnp.dot(
        spread, d_recv[...].reshape(n * slots, head_cols), preferred_element_type=F32
    )
    q_send[...] = (base[...] + update).reshape(n, block, head_cols).astype(BF16)
    q_recv[ada] = q_send[ada]

    def q_copy(target):
        return pltpu.make_async_remote_copy(
            src_ref=q_send.at[target],
            dst_ref=q_recv.at[ada],
            send_sem=qs_sem.at[target],
            recv_sem=qr_sem.at[ada],
            device_id={"ada": target},
            device_id_type=MESH,
        )

    def q_arrived(source):
        pltpu.make_async_remote_copy(
            src_ref=q_send.at[source],
            dst_ref=q_recv.at[source],
            send_sem=qs_sem.at[source],
            recv_sem=qr_sem.at[source],
            device_id={"ada": source},
            device_id_type=MESH,
        ).wait_recv()

    for target in targets:
        q_copy(target).start()

    scale = 1.0 / math.sqrt(HD)

    for source in sources:
        q_arrived(source)
    per_source = head_cols // HD
    for h in range(kv_heads):
        parts = []
        for g in range(group):
            head = h * group + g
            first = head % per_source * HD
            parts.append(q_recv[head // per_source, :, first : first + HD].astype(F32))
        query = jnp.concatenate(parts, axis=0).astype(BF16)
        lanes = slice(h * HD, (h + 1) * HD)
        scores = jnp.where(allowed, nt_dot(query, keys[:, lanes]) * scale, NEGATIVE)
        top = jnp.max(scores, axis=1, keepdims=True)
        weights = jnp.where(allowed, jnp.exp(scores - top), 0.0)
        denominator = jnp.sum(weights, axis=1, keepdims=True)
        high = weights.astype(BF16)
        low = (weights - high.astype(F32)).astype(BF16)
        both = jnp.dot(
            jnp.concatenate([high, low], axis=0), values[:, lanes], preferred_element_type=F32
        )
        attended = (both[: group * block] + both[group * block :]) / denominator
        for g in range(group):
            first = (h * group + g) * HD
            result[:, first : first + HD] = attended[g * block : (g + 1) * block]

    for t in range(steps):
        out_ref[t] = result[t * rows : (t + 1) * rows, :].astype(BF16)

    for k in range(CHUNKS):

        @pl.when(o < span - 2)
        def _():
            far_up(k).wait_send()

        @pl.when(o > 1)
        def _():
            far_down(k).wait_send()

        for line in range(span):
            across(k, line).wait_send()

            @pl.when(((line == o) | (line <= o - REACH)) & (o < span - 1))
            def _():
                upward(k, line).wait_send()

            @pl.when(((line == o) | (line >= o + REACH)) & (o > 0))
            def _():
                downward(k, line).wait_send()

            for column in range(2):
                sideways(k, line, column).wait_send()
    for d in range(1, n_dec):
        pool_send_copy(d).wait_send()
    for target in targets:
        d_copy(target).wait_send()
        q_copy(target).wait_send()


def body(
    inputs,
    query_weight,
    adapter_down,
    adapter_up,
    adapter_ids,
    new_cache,
    cache_pool,
    page_table,
    lengths,
):
    n, n_dec = lax.axis_size("ada"), lax.axis_size("dec")
    steps, rows, width = inputs.shape
    held, _, rank = adapter_down.shape
    assert held == 1 and n % 4 == 0
    head_cols = query_weight.shape[1]
    block, slots, span = steps * rows, steps * CAP, n // 4
    edges = [width // EDGES[-1] * e for e in EDGES]
    sizes = [b - a for a, b in zip(edges[:-1], edges[1:])]
    part = sizes[0]
    pool_local, _, page, kv_width = cache_pool.shape
    count = -(-(rows * page_table.shape[1] * page + block) // 16) * 16
    dma = pltpu.SemaphoreType.DMA
    vmem, smem, hbm = (
        pl.BlockSpec(memory_space=pltpu.VMEM),
        pl.BlockSpec(memory_space=pltpu.SMEM),
        pl.BlockSpec(memory_space=pl.ANY),
    )
    scratch = [
        pltpu.VMEM((n, block, sizes[k] + (LANES if k == 0 else 0)), BF16) for k in range(CHUNKS)
    ] + [
        pltpu.VMEM((width, head_cols), BF16),
        pltpu.VMEM((rank, width), BF16),
        pltpu.VMEM((rank, width), BF16),
        pltpu.VMEM((n_dec * pool_local, 2, page, kv_width), BF16),
        pltpu.VMEM((n * block, head_cols), F32),
        pltpu.VMEM((n * block, rank), F32),
        pltpu.VMEM((n, slots, head_cols), BF16),
        pltpu.VMEM((n, slots, head_cols), BF16),
        pltpu.VMEM((n, block, head_cols), BF16),
        pltpu.VMEM((n, block, head_cols), BF16),
        pltpu.VMEM((count, kv_width), BF16),
        pltpu.VMEM((count, kv_width), BF16),
        pltpu.VMEM((block, width), F32),
        dma((CHUNKS,)),
        dma,
        dma,
        dma,
        dma((n_dec,)),
        dma((n_dec,)),
        dma((CHUNKS, span + 1)),
        dma((CHUNKS, span + 1)),
        dma((CHUNKS, span)),
        dma((CHUNKS, 2 * span)),
        dma((CHUNKS, n)),
        dma((n,)),
        dma((n,)),
        dma((n,)),
        dma((n,)),
    ]
    return pl.pallas_call(
        functools.partial(kernel, n, n_dec),
        out_shape=jax.ShapeDtypeStruct((steps, rows, width), BF16),
        in_specs=[vmem, hbm, hbm, hbm, smem, vmem, hbm, smem, smem],
        out_specs=vmem,
        scratch_shapes=scratch,
        compiler_params=pltpu.CompilerParams(
            collective_id=0, has_side_effects=True, vmem_limit_bytes=60 * 1024 * 1024
        ),
    )(
        inputs,
        query_weight,
        jnp.swapaxes(adapter_down[0], 0, 1),
        adapter_up[0],
        adapter_ids[:, 0],
        new_cache,
        cache_pool,
        page_table,
        lengths,
    )


def solution(mesh):
    in_specs = (
        P(None, ("dec", "ada"), None),
        P(None, "ada"),
        P(("dec", "ada"), None, None),
        P(("dec", "ada"), None, None),
        P(("dec", "ada"), None),
        P(None, ("dec", "ada"), None, None),
        P(("dec", "ada"), None, None, None),
        P(("dec", "ada"), None),
        P(("dec", "ada")),
    )
    out_specs = P(None, ("dec", "ada"), None)
    return jax.shard_map(body, mesh=mesh, in_specs=in_specs, out_specs=out_specs, check_vma=False)
```
